32 devices in a mesh: rep: 4 (over x, core), shard: 8 (over z, y).
Axes of the slice: x: 2, y: 2, z: 4, core: 2. Of those that a mesh axis runs over, the one named last changes fastest.
Arguments:
- tokens: bfloat16 [16384, 1024], P(('rep', 'shard')), may hold values from -6 to 6
- seg_ids: int32 [16384], P('rep'), may hold values from 0 to 63, never falling along the last dimension, each value on 1 to 2048 neighbouring positions
- w_qkv: bfloat16 [1024, 3072], P('shard'), may hold values from -0.1875 to 0.1875
- w_out: bfloat16 [1024, 1024], P('shard'), may hold values from -0.75 to 0.75
- w_in: bfloat16 [1024, 5248], P('shard'), may hold values from -0.1875 to 0.1875
- w_down: bfloat16 [2624, 1024], P('shard'), may hold values from -0.125 to 0.125
- attn_gain: bfloat16 [1024], P('shard'), may hold values from 0.5 to 1.5
- ffn_gain: bfloat16 [1024], P('shard'), may hold values from 0.5 to 1.5
- cotangent: bfloat16 [16384, 1024], P(('rep', 'shard')), may hold values from -6 to 6
Outputs:
- layer_out: bfloat16 [16384, 1024], P(('rep', 'shard'))
- grad_tokens: bfloat16 [16384, 1024], P(('rep', 'shard'))
- grad_attn_gain: float32 [1024], P('shard')
- grad_ffn_gain: float32 [1024], P('shard')
- grad_qkv: float32 [1024, 3072], P('shard')
- grad_out: float32 [1024, 1024], P('shard')
- grad_in: float32 [1024, 5248], P('shard')
- grad_down: float32 [2624, 1024], P('shard')
The draws below stay inside these ranges and needn't reach their ends.
Inputs may be any that keep to these rules, and one draw needn't show every extreme that they name: `seg_ids`: ids never fall along the tokens; a document may run across sequence ends, attention stays within both.
All inputs are finite; a program needn't handle non-finite values.
Results may differ from the reference program's by a relative error of at most 0.02.
Values may be sent and summed in bfloat16 or wider, within the bound.
No kernel may reach another device: no remote copies, remote signals or barrier semaphores. Data moves between devices by JAX's collectives and lax.ppermute only.
A program may use at most 256 MiB of HBM per device.

```python
import math
import jax
import jax.numpy as jnp
import numpy as np
from jax import lax

D = 1024
HEADS = 16
HEAD_DIM = 64
FF = 2624
SEQ_LEN = 4096
TOKENS = 16384
DOCS = 64


def levels(stream_key, dims, split, low, largest):
    factor_of, own = 1.0, jax.random.fold_in(stream_key, 6)
    for dim, blocks in split:
        heights = jnp.exp(jax.random.uniform(jax.random.fold_in(own, dim), (blocks,), jnp.float32, low / len(split), largest / len(split)))
        factor_of = factor_of * jnp.repeat(heights, dims[dim] // blocks).reshape([-1 if axis == dim else 1 for axis in range(len(dims))])
    return factor_of


def split_up(amount, total, limit, skew):
    portions = [(1 << 20) // math.isqrt(grade ** skew) + 1 for grade in range(2, amount + 1)]
    surplus, counts = total - limit - (amount - 1), [1] * (amount - 1)
    while surplus > 0:
        candidates = [i for i in range(amount - 1) if counts[i] < limit]
        whole, remaining = sum([portions[i] for i in candidates]), surplus
        for i in candidates:
            extra = min(limit - counts[i], max(1, remaining * portions[i] // whole), surplus)
            counts[i] = counts[i] + extra
            surplus = surplus - extra
    return np.array([limit] + counts)


def uneven_parts(stream_key, amount, total, bound, lean):
    if amount == 2:
        one = jax.random.randint(stream_key, (), max(1, total - bound), min(bound, total - 1) + 1)
        return jnp.stack([one, total - one])
    sizes = jnp.asarray(split_up(amount, total, bound, lean), jnp.int32)
    pairs = (amount - 1) // 2
    source_of, sink = sizes[1:1 + 2 * pairs:2], sizes[2:2 + 2 * pairs:2]
    slack = jnp.minimum(source_of - 1, bound - sink)
    moved = jax.random.randint(jax.random.fold_in(stream_key, 1), (pairs,), 0, 1 << 20) % (slack + 1)
    sizes = sizes.at[1:1 + 2 * pairs:2].set(source_of - moved).at[2:2 + 2 * pairs:2].set(sink + moved)
    return sizes[jax.random.permutation(jax.random.fold_in(stream_key, 2), amount)]


def normal_values(rng, extent, deviation, reach, shards=(), kind=jnp.bfloat16):
    gain = levels(rng, extent, shards, -0.22, 0.18) if shards else 1.0
    drawn = jax.random.normal(rng, extent, jnp.float32) * deviation * gain
    return jnp.minimum(jnp.maximum(drawn, -reach), reach).astype(kind)


def setup_inputs(seed: int = 0) -> dict:
    keys = jax.random.split(jax.random.key(seed), 10)
    tokens = normal_values(keys[0], (TOKENS, D), 1.0, 6.0, ((0, 32),))
    seg_ids = jnp.searchsorted(jnp.cumsum(uneven_parts(keys[1], DOCS, TOKENS, SEQ_LEN // 2, 2)), jnp.arange(TOKENS), side="right").astype(jnp.int32)
    w_qkv = normal_values(keys[2], (D, 3 * D), D ** -0.5, 0.1875, ((0, 8),))
    w_out = normal_values(keys[3], (D, D), (D // 16) ** -0.5, 0.75, ((0, 8),))
    w_in = normal_values(keys[4], (D, 2 * FF), D ** -0.5, 0.1875, ((0, 8),))
    w_down = normal_values(keys[5], (FF, D), FF ** -0.5, 0.125, ((0, 8),))
    attn_gain = jnp.clip(1.0 + 0.1 * jax.random.normal(keys[6], (D,), jnp.float32), 0.5, 1.5).astype(jnp.bfloat16)
    ffn_gain = jnp.clip(1.0 + 0.1 * jax.random.normal(keys[7], (D,), jnp.float32), 0.5, 1.5).astype(jnp.bfloat16)
    cotangent = normal_values(keys[8], (TOKENS, D), 1.0, 6.0, ((0, 32),))
    return {"tokens": tokens, "seg_ids": seg_ids, "w_qkv": w_qkv, "w_out": w_out, "w_in": w_in, "w_down": w_down, "attn_gain": attn_gain, "ffn_gain": ffn_gain, "cotangent": cotangent}


THETA = 160000.0
EPS = 1e-05
SCALE = 0.125
MASKED = -1e+30
HIGHEST = lax.Precision.HIGHEST

@jax.custom_vjp
def low(v):
    return lax.optimization_barrier(v.astype(jnp.bfloat16)).astype(jnp.float32)

@jax.custom_vjp
def low_back(v):
    return v

def low_keep(v):
    return (low(v), None)

def low_pass(kept, grad):
    return (grad,)

def back_keep(v):
    return (v, None)

def back_low(kept, grad):
    return (low(grad),)
low.defvjp(low_keep, low_pass)
low_back.defvjp(back_keep, back_low)

def norm_rows(values, gain_vec):
    centered = values - lax.optimization_barrier(jnp.mean(values, axis=-1, keepdims=True))
    variance = lax.optimization_barrier(jnp.mean(centered * centered, axis=-1, keepdims=True))
    return centered * lax.rsqrt(variance + EPS) * gain_vec

def rotate(values, positions):
    half_size = values.shape[-1] // 2
    frequency = THETA ** (-(jnp.arange(half_size, dtype=jnp.float32) * 2.0 / values.shape[-1]))
    angles = positions.astype(jnp.float32)[:, None] * frequency[None, :]
    cosine = jnp.cos(angles)[:, None, :]
    sine_part = jnp.sin(angles)[:, None, :]
    first_half = values[..., :half_size]
    second_half = values[..., half_size:]
    return jnp.concatenate([first_half * cosine - second_half * sine_part, second_half * cosine + first_half * sine_part], axis=-1)

def forward(tokens_f, w_qkv, w_out, w_in, w_down, gain_one, gain_two, seg_ids):
    rows_all = tokens_f.shape[0]
    normed_one = low(low_back(norm_rows(tokens_f, gain_one)))
    projected = low_back(jnp.dot(normed_one, w_qkv, precision=HIGHEST))
    positions = jnp.arange(rows_all, dtype=jnp.int32) % SEQ_LEN
    query_all = low(rotate(projected[:, :D].reshape(rows_all, HEADS, HEAD_DIM), positions))
    key_all = low(rotate(projected[:, D:2 * D].reshape(rows_all, HEADS, HEAD_DIM), positions))
    value_all = low(projected[:, 2 * D:].reshape(rows_all, HEADS, HEAD_DIM))
    seq_count = rows_all // SEQ_LEN

    def one_sequence(operands):
        query_seq, key_seq, value_seq, segment = operands
        same_doc = segment[:, None] == segment[None, :]

        def attend_head(head_ops):
            query_h, key_h, value_h = head_ops
            scores = low_back(jnp.dot(query_h, key_h.T, precision=HIGHEST) * SCALE)
            scores = jnp.where(same_doc, scores, MASKED)
            probs = jax.nn.softmax(scores, axis=-1)
            return jnp.dot(low(probs), value_h, precision=HIGHEST)
        heads_out = lax.map(jax.checkpoint(attend_head), (jnp.transpose(query_seq, (1, 0, 2)), jnp.transpose(key_seq, (1, 0, 2)), jnp.transpose(value_seq, (1, 0, 2))))
        return jnp.transpose(heads_out, (1, 0, 2))
    attended = lax.map(jax.checkpoint(one_sequence), (query_all.reshape(seq_count, SEQ_LEN, HEADS, HEAD_DIM), key_all.reshape(seq_count, SEQ_LEN, HEADS, HEAD_DIM), value_all.reshape(seq_count, SEQ_LEN, HEADS, HEAD_DIM), seg_ids.reshape(seq_count, SEQ_LEN)))
    attn_low = low(low_back(attended.reshape(rows_all, D)))
    resid_mid = tokens_f + low_back(jnp.dot(attn_low, w_out, precision=HIGHEST))
    normed_two = low(low_back(norm_rows(resid_mid, gain_two)))
    pre_act = low_back(jnp.dot(normed_two, w_in, precision=HIGHEST))
    units_low = low(low_back(jax.nn.gelu(pre_act[:, :FF], approximate=False) * pre_act[:, FF:]))
    return resid_mid + low_back(jnp.dot(units_low, w_down, precision=HIGHEST))

def reference(tokens, seg_ids, w_qkv, w_out, w_in, w_down, attn_gain, ffn_gain, cotangent):
    inputs = tuple((a.astype(jnp.float32) for a in (tokens, w_qkv, w_out, w_in, w_down, attn_gain, ffn_gain)))

    def wrapped(tok_f, wq, wo, wi, wd, gone, gtwo):
        return forward(tok_f, wq, wo, wi, wd, gone, gtwo, seg_ids)
    result, pull_back = jax.vjp(wrapped, *inputs)
    grads = pull_back(cotangent.astype(jnp.float32))
    return (result.astype(jnp.bfloat16), grads[0].astype(jnp.bfloat16), grads[5], grads[6], grads[1], grads[2], grads[3], grads[4])
```

```python
import functools

import jax
import jax.numpy as jnp
from jax import lax
from jax.experimental import pallas as pl
from jax.experimental.pallas import tpu as pltpu
from jax.sharding import PartitionSpec as P

HEAD_DIM = 64
SPAN = 8
PAIR = 2 * HEAD_DIM
THETA = 160000.0
EPS = 1e-05
SCALE = 0.125
MASKED = -1e30
BLOCK = 256
BOTH = ("shard", "rep")


def norm_rows(values, gain_vec):
    centered = values - jnp.mean(values, axis=-1, keepdims=True)
    variance = jnp.mean(centered * centered, axis=-1, keepdims=True)
    return centered * lax.rsqrt(variance + EPS) * gain_vec


def gated_units(pre_act):
    units = pre_act.shape[1] // 2
    return jax.nn.gelu(pre_act[:, :units], approximate=False) * pre_act[:, units:]


def gather_weight(shard):
    copies = lax.axis_size("rep")
    mine = lax.axis_index("rep")
    rows, cols = shard.shape
    if rows % (8 * copies) == 0:
        part = lax.dynamic_slice_in_dim(shard, mine * (rows // copies), rows // copies)
        return lax.all_gather(part, BOTH, axis=0, tiled=True)
    flat = shard.reshape(rows * cols // 128, 128)
    count = flat.shape[0] // copies
    part = lax.dynamic_slice_in_dim(flat, mine * count, count)
    return lax.all_gather(part, BOTH, axis=0, tiled=True).reshape(-1, cols)


def scatter_grad(grad, rows):
    copies = lax.axis_size("rep")
    if rows % (8 * copies) == 0:
        return lax.psum_scatter(grad, BOTH, scatter_dimension=0, tiled=True)
    flat = grad.reshape(-1, 128)
    return lax.psum_scatter(flat, BOTH, scatter_dimension=0, tiled=True)


def finish_grad(share, rows):
    whole = lax.all_gather(share, "rep", axis=0, tiled=True)
    return whole.reshape(rows, -1).astype(jnp.float32)


def exchange(blocks):
    size = lax.axis_size("shard")
    groups = [list(range(first, first + SPAN)) for first in range(0, size, SPAN)]
    return lax.all_to_all(
        blocks, "shard", 0, 0, tiled=False, axis_index_groups=groups if size > SPAN else None
    )


def lanes(shape):
    return lax.broadcasted_iota(jnp.int32, shape, len(shape) - 1)


def turned(values, cosine, sine):
    lower = lanes(values.shape) % HEAD_DIM < HEAD_DIM // 2
    other = jnp.where(
        lower,
        pltpu.roll(values, PAIR - HEAD_DIM // 2, 1),
        pltpu.roll(values, HEAD_DIM // 2, 1),
    )
    return values * cosine + other * sine


def project_body(n_ref, wq_ref, wk_ref, wv_ref, cos_ref, sin_ref, out_ref):
    rows = n_ref[...]
    for part, w_ref in enumerate((wq_ref, wk_ref, wv_ref)):
        result = jnp.dot(rows, w_ref[...], preferred_element_type=jnp.float32)
        for pair in range(result.shape[1] // PAIR):
            piece = result[:, pair * PAIR : (pair + 1) * PAIR]
            if part < 2:
                piece = turned(piece, cos_ref[...], sin_ref[...])
            out_ref[pair, :, part * PAIR : (part + 1) * PAIR] = piece.astype(jnp.bfloat16)


def project(normed, weight, cosine, sine):
    rows, width = normed.shape
    step = 2
    steps = SPAN // step
    w_spec = lambda part: pl.BlockSpec(
        (width, step * PAIR), lambda d: (0, part * steps + d)
    )
    whole = lambda array: pl.BlockSpec(array.shape, lambda d: (0, 0))
    return pl.pallas_call(
        project_body,
        grid=(steps,),
        in_specs=[whole(normed), w_spec(0), w_spec(1), w_spec(2), whole(cosine), whole(sine)],
        out_specs=pl.BlockSpec((step, rows, 3 * PAIR), lambda d: (d, 0, 0)),
        out_shape=jax.ShapeDtypeStruct((SPAN, rows, 3 * PAIR), jnp.bfloat16),
        name="project_heads",
    )(normed, weight, weight, weight, cosine, sine)


def nt_dot(a, b):
    return lax.dot_general(a, b, (((1,), (1,)), ((), ())), preferred_element_type=jnp.float32)


def tn_dot(a, b):
    return lax.dot_general(a, b, (((0,), (0,)), ((), ())), preferred_element_type=jnp.float32)


def attend_body(lo_ref, hi_ref, qkv_ref, segc_ref, segr_ref, out_ref, lse_ref, acc_ref, max_ref):
    block = BLOCK
    first_head = lanes((block, PAIR)) < HEAD_DIM

    def query_step(i, _):
        at = pl.ds(pl.multiple_of(i * block, block), block)
        query = qkv_ref[at, :PAIR] * jnp.bfloat16(SCALE)
        zero = jnp.zeros_like(query)
        queries = (jnp.where(first_head, query, zero), jnp.where(first_head, zero, query))
        own = jnp.concatenate([segc_ref[at, :]] * (block // 128), axis=1)
        for head in range(2):
            acc_ref[head] = jnp.zeros((block, PAIR), jnp.float32)
            max_ref[head] = jnp.full((block, 128), MASKED, jnp.float32)

        def key_step(j, _):
            there = pl.ds(pl.multiple_of(j * block, block), block)
            key = qkv_ref[there, PAIR : 2 * PAIR]
            value = qkv_ref[there, 2 * PAIR :]
            one = jnp.ones_like(value)
            values = (jnp.where(first_head, value, one), jnp.where(first_head, one, value))
            same = own == segr_ref[0:1, there]
            for head in range(2):
                scores = jnp.where(same, nt_dot(queries[head], key), MASKED)
                before = max_ref[head]
                now = jnp.maximum(before, jnp.max(scores, axis=1, keepdims=True))
                wide = jnp.concatenate([now] * (block // 128), axis=1)
                weights = jnp.exp(scores - wide).astype(jnp.bfloat16)
                gained = jnp.dot(weights, values[head], preferred_element_type=jnp.float32)
                acc_ref[head] = acc_ref[head] * jnp.exp(before - now) + gained
                max_ref[head] = now
            return 0

        lax.fori_loop(lo_ref[i], hi_ref[i], key_step, 0)
        first, second = acc_ref[0], acc_ref[1]
        top = jnp.where(first_head, first, second)
        total = jnp.where(first_head, pltpu.roll(first, HEAD_DIM, 1), pltpu.roll(second, HEAD_DIM, 1))
        out_ref[at, :] = (top / total).astype(jnp.bfloat16)
        lse = jnp.where(first_head, max_ref[0], max_ref[1]) + jnp.log(total)
        flipped = lse.T
        lse_ref[0:1, at] = flipped[0:1]
        lse_ref[1:2, at] = flipped[HEAD_DIM : HEAD_DIM + 1]
        return 0

    lax.fori_loop(0, out_ref.shape[0] // block, query_step, 0)


def spec_smem():
    return pl.BlockSpec(memory_space=pltpu.SMEM)


def spec_vmem():
    return pl.BlockSpec(memory_space=pltpu.VMEM)


def attend(qkv, lows, highs, seg_col, seg_row):
    length = qkv.shape[0]
    return pl.pallas_call(
        attend_body,
        in_specs=[spec_smem(), spec_smem()] + [spec_vmem()] * 3,
        out_specs=[spec_vmem()] * 2,
        out_shape=[
            jax.ShapeDtypeStruct((length, PAIR), jnp.bfloat16),
            jax.ShapeDtypeStruct((8, length), jnp.float32),
        ],
        scratch_shapes=[
            pltpu.VMEM((2, BLOCK, PAIR), jnp.float32),
            pltpu.VMEM((2, BLOCK, 128), jnp.float32),
        ],
        name="attend_forward",
    )(lows, highs, qkv, seg_col, seg_row)


def attend_back_body(
    lo_ref, hi_ref, qkv_ref, out_ref, grad_ref, lse_ref, segc_ref, segr_ref, cos_ref, sin_ref,
    res_ref, dq_ref, dk_ref, dv_ref, sum_ref,
):
    block = BLOCK
    length = qkv_ref.shape[0]
    first_head = lanes((block, PAIR)) < HEAD_DIM
    sub = lax.broadcasted_iota(jnp.int32, (8, PAIR), 0)
    picks = (lanes((8, PAIR)) // HEAD_DIM == sub).astype(jnp.float32)

    def prepare(i, _):
        at = pl.ds(pl.multiple_of(i * block, block), block)
        product = grad_ref[at, :].astype(jnp.float32) * out_ref[at, :].astype(jnp.float32)
        sum_ref[:, at] = lax.dot_general(
            picks, product, (((1,), (1,)), ((), ())),
            precision=lax.Precision.HIGHEST, preferred_element_type=jnp.float32,
        )
        dq_ref[at, :] = jnp.zeros((block, PAIR), jnp.float32)
        return 0

    lax.fori_loop(0, length // block, prepare, 0)

    def key_step(j, _):
        at = pl.ds(pl.multiple_of(j * block, block), block)
        key = qkv_ref[at, PAIR : 2 * PAIR]
        value = qkv_ref[at, 2 * PAIR :]
        zero = jnp.zeros_like(key)
        keys = (jnp.where(first_head, key, zero), jnp.where(first_head, zero, key))
        own = jnp.concatenate([segc_ref[at, :]] * (block // 128), axis=1)
        dk_ref[...] = jnp.zeros((block, PAIR), jnp.float32)
        dv_ref[...] = jnp.zeros((block, PAIR), jnp.float32)

        def query_step(i, _):
            there = pl.ds(pl.multiple_of(i * block, block), block)
            query = qkv_ref[there, :PAIR] * jnp.bfloat16(SCALE)
            grad = grad_ref[there, :]
            queries = (jnp.where(first_head, query, zero), jnp.where(first_head, zero, query))
            grads = (jnp.where(first_head, grad, zero), jnp.where(first_head, zero, grad))
            same = own == segr_ref[0:1, there]
            dv, dk, dq = dv_ref[...], dk_ref[...], dq_ref[there, :]
            for head in range(2):
                scores = jnp.where(same, nt_dot(key, queries[head]), MASKED)
                weights = jnp.exp(scores - lse_ref[head : head + 1, there])
                pulled = nt_dot(value, grads[head])
                slopes = (weights * (pulled - sum_ref[head : head + 1, there])).astype(jnp.bfloat16)
                dv = dv + jnp.dot(weights.astype(jnp.bfloat16), grads[head], preferred_element_type=jnp.float32)
                dk = dk + jnp.dot(slopes, queries[head], preferred_element_type=jnp.float32)
                dq = dq + tn_dot(slopes, keys[head])
            dv_ref[...] = dv
            dk_ref[...] = dk
            dq_ref[there, :] = dq
            return 0

        lax.fori_loop(lo_ref[j], hi_ref[j], query_step, 0)
        res_ref[at, PAIR : 2 * PAIR] = turned(dk_ref[...], cos_ref[at, :], -sin_ref[at, :]).astype(jnp.bfloat16)
        res_ref[at, 2 * PAIR :] = dv_ref[...].astype(jnp.bfloat16)
        return 0

    lax.fori_loop(0, length // block, key_step, 0)

    def finish(i, _):
        at = pl.ds(pl.multiple_of(i * block, block), block)
        res_ref[at, :PAIR] = turned(dq_ref[at, :] * SCALE, cos_ref[at, :], -sin_ref[at, :]).astype(jnp.bfloat16)
        return 0

    lax.fori_loop(0, length // block, finish, 0)


def attend_back(qkv, out, grad, lse, lows, highs, seg_col, seg_row, cosine, sine):
    length = qkv.shape[0]
    return pl.pallas_call(
        attend_back_body,
        in_specs=[spec_smem(), spec_smem()] + [spec_vmem()] * 8,
        out_specs=spec_vmem(),
        out_shape=jax.ShapeDtypeStruct((length, 3 * PAIR), jnp.bfloat16),
        scratch_shapes=[
            pltpu.VMEM((length, PAIR), jnp.float32),
            pltpu.VMEM((BLOCK, PAIR), jnp.float32),
            pltpu.VMEM((BLOCK, PAIR), jnp.float32),
            pltpu.VMEM((8, length), jnp.float32),
        ],
        name="attend_backward",
    )(lows, highs, qkv, out, grad, lse, seg_col, seg_row, cosine, sine)


def local(tokens, seg_ids, w_qkv, w_out, w_in, w_down, attn_gain, ffn_gain, cotangent):
    f32, bf16 = jnp.float32, jnp.bfloat16
    rows, width = tokens.shape
    length = SPAN * rows
    position = lax.axis_index("shard")
    offset = position % SPAN

    full_qkv = gather_weight(w_qkv)
    placed = jnp.zeros((2, width), f32)
    placed = lax.dynamic_update_slice(
        placed, jnp.stack([attn_gain, ffn_gain]).astype(f32), (0, position * attn_gain.shape[0])
    )
    gains = lax.psum(placed, "shard")
    gain_one, gain_two = gains[0], gains[1]
    full_out = gather_weight(w_out)
    full_in = gather_weight(w_in)
    full_down = gather_weight(w_down)

    lane = jnp.arange(PAIR, dtype=jnp.int32)
    half = HEAD_DIM // 2
    frequency = THETA ** (-((lane % half).astype(f32) * 2.0 / HEAD_DIM))
    angles = jnp.arange(length, dtype=jnp.int32).astype(f32)[:, None] * frequency[None, :]
    cosine = jnp.cos(angles)
    sine = jnp.sin(angles) * jnp.where(lane % HEAD_DIM < half, -1.0, 1.0)
    here = offset * rows
    cosine_here = lax.dynamic_slice_in_dim(cosine, here, rows)
    sine_here = lax.dynamic_slice_in_dim(sine, here, rows)
    segments = lax.dynamic_slice_in_dim(seg_ids, (position - offset) * rows, length)
    seg_col = jnp.broadcast_to(segments[:, None], (length, 128))
    seg_row = jnp.broadcast_to(segments[None, :], (8, length))
    firsts, lasts = segments[::BLOCK], segments[BLOCK - 1 :: BLOCK]
    lows = jnp.sum(segments[None, :] < firsts[:, None], axis=1, dtype=jnp.int32) // BLOCK
    highs = (jnp.sum(segments[None, :] <= lasts[:, None], axis=1, dtype=jnp.int32) + BLOCK - 1) // BLOCK

    resid_in = tokens.astype(f32)
    normed_one = norm_rows(resid_in, gain_one).astype(bf16)
    sent = project(normed_one, full_qkv, cosine_here, sine_here)
    qkv = exchange(sent).reshape(length, 3 * PAIR)
    out_heads, lse = attend(qkv, lows, highs, seg_col, seg_row)
    attn_low = jnp.transpose(
        exchange(out_heads.reshape(SPAN, rows, PAIR)), (1, 0, 2)
    ).reshape(rows, width)
    resid_mid = resid_in + jnp.dot(attn_low, full_out, preferred_element_type=f32)

    normed_two = norm_rows(resid_mid, gain_two).astype(bf16)
    pre_act = jnp.dot(normed_two, full_in, preferred_element_type=f32)
    units_low = gated_units(pre_act).astype(bf16)
    layer_out = (resid_mid + jnp.dot(units_low, full_down, preferred_element_type=f32)).astype(bf16)

    grad_units_low = jnp.einsum("td,fd->tf", cotangent, full_down, preferred_element_type=f32).astype(bf16)
    pull_gate = jax.vjp(gated_units, pre_act)[1]
    grad_pre = pull_gate(grad_units_low.astype(f32))[0].astype(bf16)
    grad_normed_two = jnp.einsum("tf,df->td", grad_pre, full_in, preferred_element_type=f32).astype(bf16)
    pull_norm_two = jax.vjp(norm_rows, resid_mid, gain_two)[1]
    grad_mid_norm, grad_gain_two = pull_norm_two(grad_normed_two.astype(f32))
    grad_resid = cotangent.astype(f32) + grad_mid_norm
    grad_branch_low = grad_resid.astype(bf16)
    grad_attn = jnp.einsum("te,de->td", grad_branch_low, full_out, preferred_element_type=f32).astype(bf16)
    grad_heads = exchange(jnp.transpose(grad_attn.reshape(rows, SPAN, PAIR), (1, 0, 2)))
    grad_heads = grad_heads.reshape(length, PAIR)

    grad_down = jnp.einsum("tf,td->fd", units_low, cotangent, preferred_element_type=f32).astype(bf16)
    grad_in = jnp.einsum("td,tf->df", normed_two, grad_pre, preferred_element_type=f32).astype(bf16)
    grad_out = jnp.einsum("td,te->de", attn_low, grad_branch_low, preferred_element_type=f32).astype(bf16)
    share_down = scatter_grad(grad_down, w_down.shape[0])
    share_in = scatter_grad(grad_in, w_in.shape[0])
    share_out = scatter_grad(grad_out, w_out.shape[0])

    slopes = attend_back(qkv, out_heads, grad_heads, lse, lows, highs, seg_col, seg_row, cosine, sine)
    back = exchange(slopes.reshape(SPAN, rows, 3 * PAIR))
    grad_proj = jnp.transpose(back.reshape(SPAN, rows, 3, PAIR), (1, 2, 0, 3)).reshape(rows, 3 * width)
    grad_qkv = jnp.einsum("td,tf->df", normed_one, grad_proj, preferred_element_type=f32).astype(bf16)
    share_qkv = scatter_grad(grad_qkv, w_qkv.shape[0])
    grad_normed_one = jnp.einsum("tf,df->td", grad_proj, full_qkv, preferred_element_type=f32).astype(bf16)
    pull_norm_one = jax.vjp(norm_rows, resid_in, gain_one)[1]
    grad_in_norm, grad_gain_one = pull_norm_one(grad_normed_one.astype(f32))
    grad_tokens = (grad_resid + grad_in_norm).astype(bf16)

    gain_sums = lax.psum(jnp.stack([grad_gain_one, grad_gain_two]), BOTH)
    gain_rows = attn_gain.shape[0]
    gain_sums = lax.dynamic_slice_in_dim(gain_sums, position * gain_rows, gain_rows, axis=1)
    return (
        layer_out,
        grad_tokens,
        gain_sums[0],
        gain_sums[1],
        finish_grad(share_qkv, w_qkv.shape[0]),
        finish_grad(share_out, w_out.shape[0]),
        finish_grad(share_in, w_in.shape[0]),
        finish_grad(share_down, w_down.shape[0]),
    )


def solution(mesh):
    row = P(("rep", "shard"), None)
    weight = P("shard", None)
    in_specs = (row, P("rep"), weight, weight, weight, weight, P("shard"), P("shard"), row)
    out_specs = (row, row, P("shard"), P("shard"), weight, weight, weight, weight)
    return jax.shard_map(local, mesh=mesh, in_specs=in_specs, out_specs=out_specs, check_vma=False)
```

```python
import functools

import jax
import jax.numpy as jnp
from jax import lax
from jax.experimental import pallas as pl
from jax.experimental.pallas import tpu as pltpu
from jax.sharding import PartitionSpec as P

HEAD_DIM = 64
SPAN = 8
PAIR = 2 * HEAD_DIM
THETA = 160000.0
EPS = 1e-05
SCALE = 0.125
MASKED = -1e30
BLOCK = 256
BOTH = ("shard", "rep")


def norm_rows(values, gain_vec):
    centered = values - jnp.mean(values, axis=-1, keepdims=True)
    variance = jnp.mean(centered * centered, axis=-1, keepdims=True)
    return centered * lax.rsqrt(variance + EPS) * gain_vec


def gated_units(pre_act):
    units = pre_act.shape[1] // 2
    return jax.nn.gelu(pre_act[:, :units], approximate=False) * pre_act[:, units:]


def span_groups():
    size = lax.axis_size("shard")
    if size == SPAN:
        return None
    return [list(range(first, first + SPAN)) for first in range(0, size, SPAN)]


def exchange(blocks):
    return lax.all_to_all(blocks, "shard", 0, 0, tiled=False, axis_index_groups=span_groups())


def exchange_all(blocks):
    return lax.all_to_all(blocks, "shard", 0, 0, tiled=False)


def sum_copies(values):
    size = lax.axis_size("rep")
    stride = 1
    while stride < size:
        pairs = [(i, i ^ stride) for i in range(size)]
        values = values.astype(jnp.bfloat16)
        other = lax.ppermute(values, "rep", pairs)
        values = values.astype(jnp.float32) + other.astype(jnp.float32)
        stride *= 2
    return values


def sum_copies_wide(values):
    size = lax.axis_size("rep")
    stride = 1
    while stride < size:
        values = values + lax.ppermute(values, "rep", [(i, i ^ stride) for i in range(size)])
        stride *= 2
    return values


def copy_part(shard):
    copies = lax.axis_size("rep")
    count = shard.shape[0] // copies
    return lax.dynamic_slice_in_dim(shard, lax.axis_index("rep") * count, count)


def lanes(shape):
    return lax.broadcasted_iota(jnp.int32, shape, len(shape) - 1)


def turned(values, cosine, sine):
    lower = lanes(values.shape) % HEAD_DIM < HEAD_DIM // 2
    other = jnp.where(
        lower,
        pltpu.roll(values, PAIR - HEAD_DIM // 2, 1),
        pltpu.roll(values, HEAD_DIM // 2, 1),
    )
    return values * cosine + other * sine


def project_body(x_ref, gain_ref, w_ref, cos_ref, sin_ref, out_ref, n_ref):
    normed = norm_rows(x_ref[...].astype(jnp.float32), gain_ref[0:1, :]).astype(jnp.bfloat16)
    n_ref[...] = normed
    result = jnp.dot(normed, w_ref[...], preferred_element_type=jnp.float32)
    for part in range(3):
        piece = result[:, part * PAIR : (part + 1) * PAIR]
        if part < 2:
            piece = turned(piece, cos_ref[...], sin_ref[...])
        out_ref[:, part * PAIR : (part + 1) * PAIR] = piece.astype(jnp.bfloat16)


def project(tokens, gain, weight, cosine, sine):
    length, width = tokens.shape
    step = 512
    by_rows = lambda columns: pl.BlockSpec((step, columns), lambda i: (i, 0))
    whole = lambda array: pl.BlockSpec(array.shape, lambda i: (0, 0))
    return pl.pallas_call(
        project_body,
        grid=(length // step,),
        in_specs=[by_rows(width), whole(gain), whole(weight), by_rows(PAIR), by_rows(PAIR)],
        out_specs=[by_rows(3 * PAIR), by_rows(width)],
        out_shape=[
            jax.ShapeDtypeStruct((length, 3 * PAIR), jnp.bfloat16),
            jax.ShapeDtypeStruct((length, width), jnp.bfloat16),
        ],
        name="project_heads",
    )(tokens, gain, weight, cosine, sine)


def nt_dot(a, b):
    return lax.dot_general(a, b, (((1,), (1,)), ((), ())), preferred_element_type=jnp.float32)


def tn_dot(a, b):
    return lax.dot_general(a, b, (((0,), (0,)), ((), ())), preferred_element_type=jnp.float32)


def attend_body(lo_ref, hi_ref, qkv_ref, segc_ref, segr_ref, out_ref, lse_ref, acc_ref, max_ref):
    block = BLOCK
    first_head = lanes((block, PAIR)) < HEAD_DIM

    def query_step(i, _):
        at = pl.ds(pl.multiple_of(i * block, block), block)
        query = qkv_ref[at, :PAIR] * jnp.bfloat16(SCALE)
        zero = jnp.zeros_like(query)
        queries = (jnp.where(first_head, query, zero), jnp.where(first_head, zero, query))
        own = jnp.concatenate([segc_ref[at, :]] * (block // 128), axis=1)
        for head in range(2):
            acc_ref[head] = jnp.zeros((block, PAIR), jnp.float32)
            max_ref[head] = jnp.full((block, 128), MASKED, jnp.float32)

        def key_step(j, _):
            there = pl.ds(pl.multiple_of(j * block, block), block)
            key = qkv_ref[there, PAIR : 2 * PAIR]
            value = qkv_ref[there, 2 * PAIR :]
            one = jnp.ones_like(value)
            values = (jnp.where(first_head, value, one), jnp.where(first_head, one, value))
            same = own == segr_ref[0:1, there]
            for head in range(2):
                scores = jnp.where(same, nt_dot(queries[head], key), MASKED)
                before = max_ref[head]
                now = jnp.maximum(before, jnp.max(scores, axis=1, keepdims=True))
                wide = jnp.concatenate([now] * (block // 128), axis=1)
                weights = jnp.exp(scores - wide).astype(jnp.bfloat16)
                gained = jnp.dot(weights, values[head], preferred_element_type=jnp.float32)
                acc_ref[head] = acc_ref[head] * jnp.exp(before - now) + gained
                max_ref[head] = now
            return 0

        lax.fori_loop(lo_ref[i], hi_ref[i], key_step, 0)
        first, second = acc_ref[0], acc_ref[1]
        top = jnp.where(first_head, first, second)
        total = jnp.where(first_head, pltpu.roll(first, HEAD_DIM, 1), pltpu.roll(second, HEAD_DIM, 1))
        out_ref[at, :] = (top / total).astype(jnp.bfloat16)
        lse = jnp.where(first_head, max_ref[0], max_ref[1]) + jnp.log(total)
        flipped = lse.T
        lse_ref[0:1, at] = flipped[0:1]
        lse_ref[1:2, at] = flipped[HEAD_DIM : HEAD_DIM + 1]
        return 0

    lax.fori_loop(0, out_ref.shape[0] // block, query_step, 0)


def spec_smem():
    return pl.BlockSpec(memory_space=pltpu.SMEM)


def spec_vmem():
    return pl.BlockSpec(memory_space=pltpu.VMEM)


def attend(qkv, lows, highs, seg_col, seg_row):
    length = qkv.shape[0]
    return pl.pallas_call(
        attend_body,
        in_specs=[spec_smem(), spec_smem()] + [spec_vmem()] * 3,
        out_specs=[spec_vmem()] * 2,
        out_shape=[
            jax.ShapeDtypeStruct((length, PAIR), jnp.bfloat16),
            jax.ShapeDtypeStruct((8, length), jnp.float32),
        ],
        scratch_shapes=[
            pltpu.VMEM((2, BLOCK, PAIR), jnp.float32),
            pltpu.VMEM((2, BLOCK, 128), jnp.float32),
        ],
        name="attend_forward",
    )(lows, highs, qkv, seg_col, seg_row)


def attend_back_body(
    lo_ref, hi_ref, qkv_ref, out_ref, grad_ref, lse_ref, segc_ref, segr_ref, cos_ref, sin_ref,
    res_ref, dq_ref, dk_ref, dv_ref, sum_ref,
):
    block = BLOCK
    length = qkv_ref.shape[0]
    first_head = lanes((block, PAIR)) < HEAD_DIM
    sub = lax.broadcasted_iota(jnp.int32, (8, PAIR), 0)
    picks = (lanes((8, PAIR)) // HEAD_DIM == sub).astype(jnp.float32)

    def prepare(i, _):
        at = pl.ds(pl.multiple_of(i * block, block), block)
        product = grad_ref[at, :].astype(jnp.float32) * out_ref[at, :].astype(jnp.float32)
        sum_ref[:, at] = lax.dot_general(
            picks, product, (((1,), (1,)), ((), ())),
            precision=lax.Precision.HIGHEST, preferred_element_type=jnp.float32,
        )
        dq_ref[at, :] = jnp.zeros((block, PAIR), jnp.float32)
        return 0

    lax.fori_loop(0, length // block, prepare, 0)

    def key_step(j, _):
        at = pl.ds(pl.multiple_of(j * block, block), block)
        key = qkv_ref[at, PAIR : 2 * PAIR]
        value = qkv_ref[at, 2 * PAIR :]
        zero = jnp.zeros_like(key)
        keys = (jnp.where(first_head, key, zero), jnp.where(first_head, zero, key))
        own = jnp.concatenate([segc_ref[at, :]] * (block // 128), axis=1)
        dk_ref[...] = jnp.zeros((block, PAIR), jnp.float32)
        dv_ref[...] = jnp.zeros((block, PAIR), jnp.float32)

        def query_step(i, _):
            there = pl.ds(pl.multiple_of(i * block, block), block)
            query = qkv_ref[there, :PAIR] * jnp.bfloat16(SCALE)
            grad = grad_ref[there, :]
            queries = (jnp.where(first_head, query, zero), jnp.where(first_head, zero, query))
            grads = (jnp.where(first_head, grad, zero), jnp.where(first_head, zero, grad))
            same = own == segr_ref[0:1, there]
            dv, dk, dq = dv_ref[...], dk_ref[...], dq_ref[there, :]
            for head in range(2):
                scores = jnp.where(same, nt_dot(key, queries[head]), MASKED)
                weights = jnp.exp(scores - lse_ref[head : head + 1, there])
                pulled = nt_dot(value, grads[head])
                slopes = (weights * (pulled - sum_ref[head : head + 1, there])).astype(jnp.bfloat16)
                dv = dv + jnp.dot(weights.astype(jnp.bfloat16), grads[head], preferred_element_type=jnp.float32)
                dk = dk + jnp.dot(slopes, queries[head], preferred_element_type=jnp.float32)
                dq = dq + tn_dot(slopes, keys[head])
            dv_ref[...] = dv
            dk_ref[...] = dk
            dq_ref[there, :] = dq
            return 0

        lax.fori_loop(lo_ref[j], hi_ref[j], query_step, 0)
        res_ref[at, PAIR : 2 * PAIR] = turned(dk_ref[...], cos_ref[at, :], -sin_ref[at, :]).astype(jnp.bfloat16)
        res_ref[at, 2 * PAIR :] = dv_ref[...].astype(jnp.bfloat16)
        return 0

    lax.fori_loop(0, length // block, key_step, 0)

    def finish(i, _):
        at = pl.ds(pl.multiple_of(i * block, block), block)
        res_ref[at, :PAIR] = turned(dq_ref[at, :] * SCALE, cos_ref[at, :], -sin_ref[at, :]).astype(jnp.bfloat16)
        return 0

    lax.fori_loop(0, length // block, finish, 0)


def attend_back(qkv, out, grad, lse, lows, highs, seg_col, seg_row, cosine, sine):
    length = qkv.shape[0]
    return pl.pallas_call(
        attend_back_body,
        in_specs=[spec_smem(), spec_smem()] + [spec_vmem()] * 8,
        out_specs=spec_vmem(),
        out_shape=jax.ShapeDtypeStruct((length, 3 * PAIR), jnp.bfloat16),
        scratch_shapes=[
            pltpu.VMEM((length, PAIR), jnp.float32),
            pltpu.VMEM((BLOCK, PAIR), jnp.float32),
            pltpu.VMEM((BLOCK, PAIR), jnp.float32),
            pltpu.VMEM((8, length), jnp.float32),
        ],
        name="attend_backward",
    )(lows, highs, qkv, out, grad, lse, seg_col, seg_row, cosine, sine)


def local(tokens, seg_ids, w_qkv, w_out, w_in, w_down, attn_gain, ffn_gain, cotangent):
    f32, bf16 = jnp.float32, jnp.bfloat16
    rows, width = tokens.shape
    length = SPAN * rows
    shards = lax.axis_size("shard")
    position = lax.axis_index("shard")
    offset = position % SPAN
    units = w_in.shape[1] // 2

    all_tokens = lax.all_gather(
        tokens, "shard", axis=0, tiled=True, axis_index_groups=span_groups()
    )
    shard_rows = w_qkv.shape[0]
    by_pair = w_qkv.reshape(shard_rows, 3, SPAN, PAIR).transpose(2, 0, 1, 3)
    by_pair = by_pair.reshape(SPAN, shard_rows, 3 * PAIR)
    own_qkv = exchange_all(jnp.concatenate([by_pair] * (shards // SPAN), 0))
    own_qkv = own_qkv.reshape(width, 3 * PAIR)
    placed = jnp.zeros((2, width), f32)
    gain_rows = attn_gain.shape[0]
    placed = lax.dynamic_update_slice(
        placed, jnp.stack([attn_gain, ffn_gain]).astype(f32), (0, position * gain_rows)
    )
    gains = lax.psum(placed, "shard")
    gain_one, gain_two = gains[0], gains[1]
    flat_down = w_down.reshape(shard_rows, -1)
    wide = copy_part(jnp.concatenate([w_in, w_out, flat_down], axis=1))
    full = lax.all_gather(wide, BOTH, axis=0, tiled=True)
    full_in = full[:, : 2 * units]
    full_out = full[:, 2 * units : 2 * units + width]
    full_down = full[:, 2 * units + width :].reshape(units, width)
    full_qkv = lax.all_gather(copy_part(w_qkv), BOTH, axis=0, tiled=True)

    lane = jnp.arange(PAIR, dtype=jnp.int32)
    half = HEAD_DIM // 2
    frequency = THETA ** (-((lane % half).astype(f32) * 2.0 / HEAD_DIM))
    angles = jnp.arange(length, dtype=jnp.int32).astype(f32)[:, None] * frequency[None, :]
    cosine = jnp.cos(angles)
    sine = jnp.sin(angles) * jnp.where(lane % HEAD_DIM < half, -1.0, 1.0)
    segments = lax.dynamic_slice_in_dim(seg_ids, (position - offset) * rows, length)
    seg_col = jnp.broadcast_to(segments[:, None], (length, 128))
    seg_row = jnp.broadcast_to(segments[None, :], (8, length))
    firsts, lasts = segments[::BLOCK], segments[BLOCK - 1 :: BLOCK]
    lows = jnp.sum(segments[None, :] < firsts[:, None], axis=1, dtype=jnp.int32) // BLOCK
    highs = (jnp.sum(segments[None, :] <= lasts[:, None], axis=1, dtype=jnp.int32) + BLOCK - 1) // BLOCK

    qkv, all_normed = project(all_tokens, jnp.broadcast_to(gain_one, (8, width)), own_qkv, cosine, sine)
    out_heads, lse = attend(qkv, lows, highs, seg_col, seg_row)
    attn_low = jnp.transpose(
        exchange(out_heads.reshape(SPAN, rows, PAIR)), (1, 0, 2)
    ).reshape(rows, width)
    resid_in = tokens.astype(f32)
    resid_mid = resid_in + jnp.dot(attn_low, full_out, preferred_element_type=f32)

    normed_two = norm_rows(resid_mid, gain_two).astype(bf16)
    pre_act = jnp.dot(normed_two, full_in, preferred_element_type=f32)
    units_low = gated_units(pre_act).astype(bf16)
    layer_out = (resid_mid + jnp.dot(units_low, full_down, preferred_element_type=f32)).astype(bf16)

    grad_units_low = jnp.einsum("td,fd->tf", cotangent, full_down, preferred_element_type=f32).astype(bf16)
    pull_gate = jax.vjp(gated_units, pre_act)[1]
    grad_pre = pull_gate(grad_units_low.astype(f32))[0].astype(bf16)
    grad_normed_two = jnp.einsum("tf,df->td", grad_pre, full_in, preferred_element_type=f32).astype(bf16)
    pull_norm_two = jax.vjp(norm_rows, resid_mid, gain_two)[1]
    grad_mid_norm, grad_gain_two = pull_norm_two(grad_normed_two.astype(f32))
    grad_resid = cotangent.astype(f32) + grad_mid_norm
    grad_branch_low = grad_resid.astype(bf16)
    grad_attn = jnp.einsum("te,de->td", grad_branch_low, full_out, preferred_element_type=f32).astype(bf16)
    grad_heads = exchange(jnp.transpose(grad_attn.reshape(rows, SPAN, PAIR), (1, 0, 2)))
    grad_heads = grad_heads.reshape(length, PAIR)

    grad_down = jnp.einsum("tf,td->fd", units_low, cotangent, preferred_element_type=f32).astype(bf16)
    grad_in = jnp.einsum("td,tf->df", normed_two, grad_pre, preferred_element_type=f32).astype(bf16)
    grad_out = jnp.einsum("td,te->de", attn_low, grad_branch_low, preferred_element_type=f32).astype(bf16)
    grads = jnp.concatenate([grad_in, grad_out, grad_down.reshape(width, units)], axis=1)
    share = lax.psum_scatter(grads, BOTH, scatter_dimension=0, tiled=True)

    slopes = attend_back(qkv, out_heads, grad_heads, lse, lows, highs, seg_col, seg_row, cosine, sine)
    back = exchange(slopes.reshape(SPAN, rows, 3 * PAIR))
    own_grad = jnp.einsum("td,tf->df", all_normed, slopes, preferred_element_type=f32).astype(bf16)
    own_grad = exchange_all(own_grad.reshape(shards, shard_rows, 3 * PAIR))
    own_grad = own_grad.reshape(shards // SPAN, SPAN, shard_rows, 3, PAIR)
    if shards == SPAN:
        own_grad = own_grad[0]
    else:
        own_grad = jnp.sum(own_grad.astype(f32), axis=0)
    own_grad = sum_copies(own_grad)
    grad_qkv = own_grad.transpose(1, 2, 0, 3).reshape(shard_rows, 3 * width).astype(f32)
    grad_proj = jnp.transpose(back.reshape(SPAN, rows, 3, PAIR), (1, 2, 0, 3)).reshape(rows, 3 * width)
    grad_normed_one = jnp.einsum("tf,df->td", grad_proj, full_qkv, preferred_element_type=f32).astype(bf16)
    pull_norm_one = jax.vjp(norm_rows, resid_in, gain_one)[1]
    grad_in_norm, grad_gain_one = pull_norm_one(grad_normed_one.astype(f32))
    grad_tokens = (grad_resid + grad_in_norm).astype(bf16)

    gain_parts = jnp.stack([grad_gain_one, grad_gain_two]).reshape(2, shards, gain_rows)
    gain_parts = exchange_all(jnp.transpose(gain_parts, (1, 0, 2)))
    gain_sums = sum_copies_wide(jnp.sum(gain_parts, axis=0))
    done = lax.all_gather(share, "rep", axis=0, tiled=True)
    return (
        layer_out,
        grad_tokens,
        gain_sums[0],
        gain_sums[1],
        grad_qkv,
        done[:, 2 * units : 2 * units + width].astype(f32),
        done[:, : 2 * units].astype(f32),
        done[:, 2 * units + width :].reshape(w_down.shape).astype(f32),
    )


def solution(mesh):
    row = P(("rep", "shard"), None)
    weight = P("shard", None)
    in_specs = (row, P("rep"), weight, weight, weight, weight, P("shard"), P("shard"), row)
    out_specs = (row, row, P("shard"), P("shard"), weight, weight, weight, weight)
    return jax.shard_map(local, mesh=mesh, in_specs=in_specs, out_specs=out_specs, check_vma=False)
```
